512 devices in a mesh: uv: 16 (over x_hi, z), chan: 32 (over y, x_lo, core).
Axes of the slice: x: 4 (x_hi: 2, x_lo: 2; x = x_hi * 2 + x_lo), y: 8, z: 8, core: 2. Of those that a mesh axis runs over, the one named last changes fastest.
Arguments:
- visibility: bfloat16 [2, 512, 128, 4096], P(None, 'chan', 'uv'), may hold values from -6 to 6
- eigen_basis: bfloat16 [512, 512], P('chan'), may hold values from -0.25 to 0.25
- eigenvalues: float32 [512], replicated, may hold values from 0.01 to 100
- noise_power: float32 [128], P('uv'), may hold values from 0.1 to 10
Outputs:
- image_cube: bfloat16 [2, 512, 128, 4096], P(None, ('uv', 'chan'))
The draws below stay inside these ranges and needn't reach their ends.
All inputs are finite; a program needn't handle non-finite values.
Results may differ from the reference program's by a relative error of at most 0.019.
Values may be sent and summed in bfloat16 or wider, within the bound.
A program may use at most 64 MiB of HBM per device.

```python
import math
import jax
import jax.numpy as jnp
from jax import lax

NCH = 512
NV = 4096
ROWS = 128


def level_of(key, dims, cuts, low, largest):
    gain = 1.0
    for axis_at, blocks in cuts:
        steps = jax.random.uniform(jax.random.fold_in(jax.random.fold_in(key, 6), axis_at), (blocks,), jnp.float32, low / len(cuts), largest / len(cuts))
        gain = gain * jnp.repeat(jnp.exp(steps), dims[axis_at] // blocks).reshape((-1,) + (1,) * (len(dims) - 1 - axis_at))
    return gain


def normal_values(stream_key, dims, width, limit, split=(), kind=jnp.bfloat16):
    factor_of = level_of(stream_key, dims, split, -0.22, 0.18) if split else 1.0
    result = jax.random.normal(stream_key, dims, jnp.float32) * width * factor_of
    return jnp.minimum(jnp.maximum(result, -limit), limit).astype(kind)


def setup_inputs(seed: int = 0) -> dict:
    key_list = jax.random.split(jax.random.key(seed), 5)
    return {
        "visibility": normal_values(key_list[0], (2, NCH, ROWS, NV), 1.0, 6.0, ((1, 32), (2, 16))),
        "eigen_basis": normal_values(key_list[1], (NCH, NCH), NCH ** -0.5, 0.25, ((0, 32),)),
        "eigenvalues": jnp.clip(jnp.exp(jax.random.uniform(key_list[2], (NCH,), jnp.float32, math.log(0.01), math.log(100.0))), 0.01, 100.0),
        "noise_power": jnp.clip(jnp.exp(math.log(10.0) - 4.6051702 * jax.random.uniform(key_list[3], (ROWS,), jnp.float32) ** level_of(key_list[3], (ROWS,), ((0, 16),), -0.2, 0.2)), 0.1, 10.0),
    }


def reference(visibility, eigen_basis, eigenvalues, noise_power):
    broad_basis = eigen_basis.astype(jnp.float32)

    def clean_row(row_index):
        slab_line_row = lax.dynamic_index_in_dim(visibility, row_index, 2, keepdims=False)
        noise_level = lax.dynamic_index_in_dim(noise_power, row_index, 0, keepdims=False)
        mode_amplitudes = jnp.einsum("wj,lwr->ljr", broad_basis, slab_line_row.astype(jnp.float32)).astype(jnp.bfloat16)
        mode_filter_gain = eigenvalues / (eigenvalues + noise_level)
        foreground_signal = (mode_filter_gain[None, :, None] * mode_amplitudes.astype(jnp.float32)).astype(jnp.bfloat16)
        rearranged_slab = jnp.einsum("fq,tqj->tfj", broad_basis, foreground_signal.astype(jnp.float32))
        return (slab_line_row.astype(jnp.float32) - rearranged_slab).astype(jnp.bfloat16)

    cleaned = lax.map(clean_row, jnp.arange(visibility.shape[2], dtype=jnp.int32))

    def image_plane(chan_index):
        one_plane = lax.dynamic_index_in_dim(cleaned, chan_index, 2, keepdims=False)
        complex_plane = lax.complex(one_plane[:, 0].astype(jnp.float32), one_plane[:, 1].astype(jnp.float32))
        imaged = jnp.fft.ifft2(complex_plane, norm="ortho")
        return jnp.stack([jnp.real(imaged), jnp.imag(imaged)]).astype(jnp.bfloat16)

    planes = lax.map(image_plane, jnp.arange(visibility.shape[1], dtype=jnp.int32))
    return jnp.transpose(planes, (1, 0, 2, 3))
```

```python
import functools
import math

import jax
import jax.numpy as jnp
import numpy as np
from jax import lax
from jax.experimental import pallas as pl
from jax.experimental.pallas import tpu as pltpu
from jax.sharding import PartitionSpec as P

MESH = pl.DeviceIdType.MESH
LANES = 128
QUAD = 4
NT = (((1,), (1,)), ((), ()))


def ring_offset(step):
    return ((step + 1) // 2) * (1 if step % 2 else -1)


def clean_kernel(uv_count, chan_count, vis, eb, gain, z, d_in, work, c_out, mid, basis, basis_t, gains,
                 s_vis, r_vis, s_eb, r_eb, s_back, r_back, s_fin, r_fin):
    uv = lax.axis_index("uv")
    ch = lax.axis_index("chan")
    ring = chan_count // QUAD
    y, q = ch // QUAD, ch % QUAD
    c_loc = vis.shape[1]
    rows = vis.shape[2]
    zring = uv_count // 2
    xh, zz = uv // zring, uv % zring

    def chan_peer(step, m):
        return ((y + ring_offset(step) + ring) % ring) * QUAD + (q + m) % QUAD

    def uv_peer(step, m):
        return ((xh + m) % 2) * zring + (zz + ring_offset(step) + zring) % zring

    chan_steps = [(t, m) for t in range(ring) for m in range(QUAD)]
    uv_steps = [(t, m) for t in range(zring) for m in range(2)]

    barrier = pltpu.get_barrier_semaphore()
    for t, m in chan_steps[1:]:
        pl.semaphore_signal(barrier, inc=1, device_id=(uv, chan_peer(t, m)), device_id_type=MESH)
    for t, m in uv_steps[1:]:
        pl.semaphore_signal(barrier, inc=1, device_id=(uv_peer(t, m), ch), device_id_type=MESH)
    pl.semaphore_wait(barrier, chan_count - 1 + uv_count - 1)

    for t in range(1, ring):
        pltpu.make_async_remote_copy(
            eb, basis.at[y, q], s_eb.at[0], r_eb.at[0], device_id=(uv, chan_peer(t, 0)), device_id_type=MESH
        ).start()
    pltpu.make_async_copy(eb, basis.at[y, q], r_eb.at[0]).start()

    for s in range(2):
        for t, m in chan_steps[1:]:
            p = chan_peer(t, m)
            pltpu.make_async_remote_copy(
                vis.at[s, :, :, pl.ds(pl.multiple_of(p * LANES, LANES), LANES)],
                d_in.at[s, pl.ds(ch * c_loc, c_loc)],
                s_vis, r_vis.at[s], device_id=(uv, p), device_id_type=MESH,
            ).start()
        pltpu.make_async_copy(
            vis.at[s, :, :, pl.ds(pl.multiple_of(ch * LANES, LANES), LANES)],
            d_in.at[s, pl.ds(ch * c_loc, c_loc)],
            r_vis.at[s],
        ).start()

    for u in range(rows):
        gains[u] = jnp.broadcast_to(gain[:, u:u + 1], gains.shape[1:])

    pltpu.make_async_copy(basis.at[:, q], basis.at[:, q], r_eb.at[0]).wait()
    for m in range(1, QUAD):
        pltpu.make_async_remote_copy(
            basis.at[:, q], basis.at[:, q], s_eb.at[1], r_eb.at[1],
            device_id=(uv, chan_peer(0, m)), device_id_type=MESH,
        ).start()
    pltpu.make_async_copy(basis.at[:, pl.ds(0, QUAD - 1)], basis.at[:, pl.ds(0, QUAD - 1)], r_eb.at[1]).wait()
    nch = basis_t.shape[0]
    basis_t[...] = jnp.transpose(basis[...].reshape(nch, nch).astype(jnp.float32)).astype(jnp.bfloat16)

    for s in range(2):
        pltpu.make_async_copy(d_in.at[s], d_in.at[s], r_vis.at[s]).wait()
        work[...] = d_in[s].astype(jnp.float32).reshape(nch * rows, LANES)

        def clean_pair(pair, carry):
            first = pl.ds(2 * pair, nch, stride=rows)
            second = pl.ds(2 * pair + 1, nch, stride=rows)
            cells = jnp.concatenate([work[first, :], work[second, :]], axis=1)
            amps = jnp.dot(basis_t[...], cells.astype(jnp.bfloat16), preferred_element_type=jnp.float32)
            gain_pair = jnp.concatenate([gains[2 * pair], gains[2 * pair + 1]], axis=1)
            fore = (gain_pair * amps.astype(jnp.bfloat16).astype(jnp.float32)).astype(jnp.bfloat16)
            slab = jnp.dot(basis[...].reshape(nch, nch), fore, preferred_element_type=jnp.float32)
            left = cells - slab
            work[first, :] = left[:, :LANES]
            work[second, :] = left[:, LANES:]
            return carry

        lax.fori_loop(0, rows // 2, clean_pair, 0)
        c_out[s] = work[...].astype(jnp.bfloat16).reshape(c_out.shape[1:])

        for t, m in chan_steps[1:]:
            p = chan_peer(t, m)
            pltpu.make_async_remote_copy(
                c_out.at[s, :, p],
                mid.at[s, :, :, pl.ds(pl.multiple_of(ch * LANES, LANES), LANES)],
                s_back, r_back.at[s, y], device_id=(uv, p), device_id_type=MESH,
            ).start()
        pltpu.make_async_copy(
            c_out.at[s, :, ch],
            mid.at[s, :, :, pl.ds(pl.multiple_of(ch * LANES, LANES), LANES)],
            r_back.at[s, y],
        ).start()

    width = QUAD * LANES
    for s in range(2):
        for t in range(ring):
            src = (y + ring_offset(t) + ring) % ring
            cols = pl.ds(pl.multiple_of(src * width, width), width)
            pltpu.make_async_copy(mid.at[s, :, :, cols], mid.at[s, :, :, cols], r_back.at[s, src]).wait()
            for tt, m in uv_steps[1:]:
                p = uv_peer(tt, m)
                pltpu.make_async_remote_copy(
                    mid.at[s, p, :, cols], z.at[s, pl.ds(pl.multiple_of(uv * rows, rows), rows), cols],
                    s_fin, r_fin, device_id=(p, ch), device_id_type=MESH,
                ).start()
            pltpu.make_async_copy(
                mid.at[s, uv, :, cols], z.at[s, pl.ds(pl.multiple_of(uv * rows, rows), rows), cols], r_fin
            ).start()

    pltpu.make_async_copy(z, z, r_fin).wait()
    others = d_in.at[:, pl.ds(0, (chan_count - 1) * c_loc)]
    pltpu.make_async_copy(others, others, s_vis).wait()
    others = c_out.at[:, :, pl.ds(0, chan_count - 1)]
    pltpu.make_async_copy(others, others, s_back).wait()
    others = mid.at[:, pl.ds(0, uv_count - 1)]
    pltpu.make_async_copy(others, others, s_fin).wait()
    others = basis.at[pl.ds(0, ring - 1), 0]
    pltpu.make_async_copy(others, others, s_eb.at[0]).wait()
    others = basis.at[:, pl.ds(0, QUAD - 1)]
    pltpu.make_async_copy(others, others, s_eb.at[1]).wait()


def exchange_and_clean(visibility, eigen_basis, gain, uv_count, chan_count):
    _, c_loc, rows, nv = visibility.shape
    nch = c_loc * chan_count
    bf16, f32 = jnp.bfloat16, jnp.float32
    vmem = pl.BlockSpec(memory_space=pltpu.VMEM)
    dma = pltpu.SemaphoreType.DMA
    return pl.pallas_call(
        functools.partial(clean_kernel, uv_count, chan_count),
        out_shape=jax.ShapeDtypeStruct((2, rows * uv_count, nv), bf16),
        in_specs=[pl.BlockSpec(memory_space=pl.ANY), vmem, vmem],
        out_specs=vmem,
        scratch_shapes=[
            pltpu.VMEM((2, nch, rows, LANES), bf16),
            pltpu.VMEM((nch * rows, LANES), f32),
            pltpu.VMEM((2, uv_count, chan_count, rows, LANES), bf16),
            pltpu.VMEM((2, uv_count, rows, nv), bf16),
            pltpu.VMEM((chan_count // QUAD, QUAD, c_loc, nch), bf16),
            pltpu.VMEM((nch, nch), bf16),
            pltpu.VMEM((rows, nch, LANES), f32),
            dma, dma((2,)), dma((2,)), dma((2,)), dma, dma((2, chan_count // QUAD)), dma, dma,
        ],
        compiler_params=pltpu.CompilerParams(collective_id=0, has_side_effects=True),
        name="exchange_clean",
    )(visibility, eigen_basis, gain)


def turn(value, num, den):
    re, im = value
    num %= den
    eighth = 8 * num
    if num == 0:
        return re, im
    if eighth == 2 * den:
        return -im, re
    if eighth == 4 * den:
        return -re, -im
    if eighth == 6 * den:
        return im, -re
    angle = 2.0 * math.pi * num / den
    c, s = math.cos(angle), math.sin(angle)
    return re * c - im * s, re * s + im * c


def add(a, b):
    return a[0] + b[0], a[1] + b[1]


def sub(a, b):
    return a[0] - b[0], a[1] - b[1]


def inverse_fft(values):
    n = len(values)
    if n == 1:
        return values
    if n == 2:
        return [add(*values), sub(*values)]
    if n % 4 == 0 and n != 8:
        parts = [inverse_fft(values[k::4]) for k in range(4)]
        out = [None] * n
        for j in range(n // 4):
            a, b, c, d = (turn(parts[k][j], k * j, n) for k in range(4))
            ac, bd = add(a, c), add(b, d)
            am, bm = sub(a, c), turn(sub(b, d), 1, 4)
            out[j], out[j + n // 2] = add(ac, bd), sub(ac, bd)
            out[j + n // 4], out[j + 3 * n // 4] = add(am, bm), sub(am, bm)
        return out
    even, odd = inverse_fft(values[0::2]), inverse_fft(values[1::2])
    out = [None] * n
    for j in range(n // 2):
        o = turn(odd[j], j, n)
        out[j], out[j + n // 2] = add(even[j], o), sub(even[j], o)
    return out


def image_kernel(z, fb, fu, tw, out, t_re, t_im, y_re, y_im, buf, sem):
    rows, nv = z.shape[1], z.shape[2]
    outer = nv // LANES

    def outer_stage(block, carry):
        r = pl.ds(pl.multiple_of(block * 8, 8), 8)
        values = [
            tuple(z[s, r, a * LANES:(a + 1) * LANES].astype(jnp.float32) for s in range(2)) for a in range(outer)
        ]
        for j, (re, im) in enumerate(inverse_fft(values)):
            if j:
                c, s = tw[0, j:j + 1, :], tw[1, j:j + 1, :]
                re, im = re * c - im * s, re * s + im * c
            t_re[j, r, :] = re
            t_im[j, r, :] = im
        return carry

    lax.fori_loop(0, rows // 8, outer_stage, 0)

    def inner_stage(pair, carry):
        cells = jnp.concatenate(
            [jnp.concatenate([t_re[2 * pair + k], t_im[2 * pair + k]], axis=1) for k in range(2)], axis=0
        ).astype(jnp.bfloat16)
        res = lax.dot_general(fb[...], cells, NT, preferred_element_type=jnp.float32)
        for k in range(2):
            to = pl.ds(2 * pair + k, LANES, stride=outer)
            y_re[to, :] = res[:LANES, k * rows:(k + 1) * rows]
            y_im[to, :] = res[LANES:, k * rows:(k + 1) * rows]
        return carry

    lax.fori_loop(0, outer // 2, inner_stage, 0)

    wide = 2 * LANES

    def row_stage(block, carry):
        r = pl.ds(pl.multiple_of(block * wide, wide), wide)
        cells = jnp.concatenate([y_re[r, :], y_im[r, :]], axis=1).astype(jnp.bfloat16)
        res = lax.dot_general(fu[...], cells, NT, preferred_element_type=jnp.float32).astype(jnp.bfloat16)
        buf[0, :, r] = res[:rows]
        buf[1, :, r] = res[rows:]
        pltpu.make_async_copy(buf.at[:, :, r], out.at[:, 0, :, r], sem).start()
        return carry

    lax.fori_loop(0, nv // wide, row_stage, 0)
    pltpu.make_async_copy(buf, out.at[:, 0], sem).wait()


def dft_matrix(n, scale):
    idx = np.outer(np.arange(n), np.arange(n)) % n
    c, s = np.cos(2 * np.pi * idx / n) * scale, np.sin(2 * np.pi * idx / n) * scale
    return np.block([[c, -s], [s, c]])


def image(z):
    _, rows, nv = z.shape
    outer = nv // LANES
    bf16, f32 = jnp.bfloat16, jnp.float32
    fb = jnp.asarray(dft_matrix(LANES, 1.0), bf16)
    fu = jnp.asarray(dft_matrix(rows, 1.0 / math.sqrt(rows * nv)), bf16)
    angle = 2 * np.pi * np.outer(np.arange(outer), np.arange(LANES)) / nv
    tw = jnp.asarray(np.stack([np.cos(angle), np.sin(angle)]), f32)
    vmem = pl.BlockSpec(memory_space=pltpu.VMEM)
    return pl.pallas_call(
        image_kernel,
        out_shape=jax.ShapeDtypeStruct((2, 1, rows, nv), bf16),
        in_specs=[vmem] * 4,
        out_specs=pl.BlockSpec(memory_space=pl.ANY),
        scratch_shapes=[
            pltpu.VMEM((outer, rows, LANES), f32), pltpu.VMEM((outer, rows, LANES), f32),
            pltpu.VMEM((nv, rows), f32), pltpu.VMEM((nv, rows), f32),
            pltpu.VMEM((2, rows, nv), bf16), pltpu.SemaphoreType.DMA,
        ],
        name="image",
    )(z, fb, fu, tw)


def shards(visibility, eigen_basis, eigenvalues, noise_power):
    gain = eigenvalues[:, None] / (eigenvalues[:, None] + noise_power[None, :])
    z = exchange_and_clean(visibility, eigen_basis, gain, lax.axis_size("uv"), lax.axis_size("chan"))
    return image(z)


def solution(mesh):
    in_specs = (P(None, "chan", "uv", None), P("chan", None), P(), P("uv"))
    out_specs = P(None, ("uv", "chan"), None, None)
    return jax.shard_map(shards, mesh=mesh, in_specs=in_specs, out_specs=out_specs, check_vma=False)
```

```python
import functools
import math

import jax
import jax.numpy as jnp
import numpy as np
from jax import lax
from jax.experimental import pallas as pl
from jax.experimental.pallas import tpu as pltpu
from jax.sharding import PartitionSpec as P

MESH = pl.DeviceIdType.MESH
LANES = 128
INNER = 8
PAD = 4
QUAD = 4


def ring_offset(step):
    return ((step + 1) // 2) * (1 if step % 2 else -1)


def clean_kernel(uv_count, chan_count, vis, eb, values, noise, z, d_in, work, c_out, mid, basis, basis_t, gains,
                 s_vis, r_vis, s_eb, r_eb, s_back, r_back, s_fin, r_fin):
    uv = lax.axis_index("uv")
    ch = lax.axis_index("chan")
    ring = chan_count // QUAD
    y, q = ch // QUAD, ch % QUAD
    c_loc = vis.shape[1]
    rows = vis.shape[2]
    zring = uv_count // 2
    xh, zz = uv // zring, uv % zring

    def chan_peer(step, m):
        return ((y + ring_offset(step) + ring) % ring) * QUAD + (q + m) % QUAD

    def uv_peer(step, m):
        return ((xh + m) % 2) * zring + (zz + ring_offset(step) + zring) % zring

    chan_steps = [(t, m) for t in range(ring) for m in range(QUAD)]
    uv_steps = [(0, 0)] + [(t, m) for t in reversed(range(zring)) for m in range(2) if t or m]

    barrier = pltpu.get_barrier_semaphore()
    for t, m in chan_steps[1:]:
        pl.semaphore_signal(barrier, inc=1, device_id=(uv, chan_peer(t, m)), device_id_type=MESH)
    for t, m in uv_steps[1:]:
        pl.semaphore_signal(barrier, inc=1, device_id=(uv_peer(t, m), ch), device_id_type=MESH)
    pl.semaphore_wait(barrier, chan_count - 1 + uv_count - 1)

    for t in range(1, ring):
        pltpu.make_async_remote_copy(
            eb, basis.at[y, q], s_eb.at[0], r_eb.at[0], device_id=(uv, chan_peer(t, 0)), device_id_type=MESH
        ).start()
    pltpu.make_async_copy(eb, basis.at[y, q], r_eb.at[0]).start()

    def send_vis(s, steps):
        for t, m in steps:
            p = chan_peer(t, m)
            src = vis.at[s, :, :, pl.ds(pl.multiple_of(p * LANES, LANES), LANES)]
            dst = d_in.at[s, pl.ds(ch * c_loc, c_loc)]
            if (t, m) == (0, 0):
                pltpu.make_async_copy(src, dst, r_vis.at[s]).start()
            else:
                pltpu.make_async_remote_copy(
                    src, dst, s_vis, r_vis.at[s], device_id=(uv, p), device_id_type=MESH
                ).start()

    for s in range(2):
        send_vis(s, chan_steps)

    nch = basis_t.shape[0]
    spread = jnp.transpose(jnp.broadcast_to(values[...], (LANES, nch)))
    for u in range(rows):
        gains[u] = spread / (spread + noise[u])

    pltpu.make_async_copy(basis.at[:, q], basis.at[:, q], r_eb.at[0]).wait()
    for m in range(1, QUAD):
        pltpu.make_async_remote_copy(
            basis.at[:, q], basis.at[:, q], s_eb.at[1], r_eb.at[1],
            device_id=(uv, chan_peer(0, m)), device_id_type=MESH,
        ).start()
    pltpu.make_async_copy(basis.at[:, pl.ds(0, QUAD - 1)], basis.at[:, pl.ds(0, QUAD - 1)], r_eb.at[1]).wait()
    basis_t[...] = jnp.transpose(basis[...].reshape(nch, nch).astype(jnp.float32)).astype(jnp.bfloat16)

    def clean(s):
        pltpu.make_async_copy(d_in.at[s], d_in.at[s], r_vis.at[s]).wait()
        work[...] = d_in[s].astype(jnp.float32).reshape(nch * rows, LANES)

        def clean_pair(pair, carry):
            first = pl.ds(2 * pair, nch, stride=rows)
            second = pl.ds(2 * pair + 1, nch, stride=rows)
            cells = jnp.concatenate([work[first, :], work[second, :]], axis=1)
            amps = jnp.dot(basis_t[...], cells.astype(jnp.bfloat16), preferred_element_type=jnp.float32)
            gain_pair = jnp.concatenate([gains[2 * pair], gains[2 * pair + 1]], axis=1)
            fore = (gain_pair * amps.astype(jnp.bfloat16).astype(jnp.float32)).astype(jnp.bfloat16)
            slab = jnp.dot(basis[...].reshape(nch, nch), fore, preferred_element_type=jnp.float32)
            left = cells - slab
            work[first, :] = left[:, :LANES]
            work[second, :] = left[:, LANES:]
            return carry

        lax.fori_loop(0, rows // 2, clean_pair, 0)
        c_out[s] = work[...].astype(jnp.bfloat16).reshape(c_out.shape[1:])

    def send_back(s, steps):
        for t, m in steps:
            p = chan_peer(t, m)
            src = c_out.at[s, :, p]
            dst = mid.at[s, :, :, pl.ds(pl.multiple_of(ch * LANES, LANES), LANES)]
            if (t, m) == (0, 0):
                pltpu.make_async_copy(src, dst, r_back.at[s, y]).start()
            else:
                pltpu.make_async_remote_copy(
                    src, dst, s_back, r_back.at[s, y], device_id=(uv, p), device_id_type=MESH
                ).start()

    width = QUAD * LANES

    def relay(s, t):
        src = (y + ring_offset(t) + ring) % ring
        cols = pl.ds(pl.multiple_of(src * width, width), width)
        to = z.at[s, pl.ds(pl.multiple_of(uv * rows, rows), rows), cols]
        pltpu.make_async_copy(mid.at[s, :, :, cols], mid.at[s, :, :, cols], r_back.at[s, src]).wait()
        for tt, m in uv_steps[1:]:
            p = uv_peer(tt, m)
            pltpu.make_async_remote_copy(
                mid.at[s, p, :, cols], to, s_fin, r_fin, device_id=(p, ch), device_id_type=MESH
            ).start()
        pltpu.make_async_copy(mid.at[s, uv, :, cols], to, r_fin).start()

    for s in range(2):
        clean(s)
        send_back(s, chan_steps)
    for s in range(2):
        for t in range(ring):
            relay(s, t)

    pltpu.make_async_copy(z, z, r_fin).wait()
    for gone, sem in (
        (d_in.at[:, pl.ds(0, (chan_count - 1) * c_loc)], s_vis),
        (c_out.at[:, :, pl.ds(0, chan_count - 1)], s_back),
        (mid.at[:, pl.ds(0, uv_count - 1)], s_fin),
        (basis.at[pl.ds(0, ring - 1), 0], s_eb.at[0]),
        (basis.at[:, pl.ds(0, QUAD - 1)], s_eb.at[1]),
    ):
        pltpu.make_async_copy(gone, gone, sem).wait()


def exchange_and_clean(visibility, eigen_basis, eigenvalues, noise_power, uv_count, chan_count):
    _, c_loc, rows, nv = visibility.shape
    nch = c_loc * chan_count
    bf16, f32 = jnp.bfloat16, jnp.float32
    vmem = pl.BlockSpec(memory_space=pltpu.VMEM)
    dma = pltpu.SemaphoreType.DMA
    return pl.pallas_call(
        functools.partial(clean_kernel, uv_count, chan_count),
        out_shape=jax.ShapeDtypeStruct((2, rows * uv_count, nv), bf16),
        in_specs=[pl.BlockSpec(memory_space=pl.ANY), vmem, vmem, pl.BlockSpec(memory_space=pltpu.SMEM)],
        out_specs=pl.BlockSpec(memory_space=pl.ANY),
        scratch_shapes=[
            pltpu.VMEM((2, nch, rows, LANES), bf16),
            pltpu.VMEM((nch * rows, LANES), f32),
            pltpu.VMEM((2, uv_count, chan_count, rows, LANES), bf16),
            pltpu.VMEM((2, uv_count, rows, nv), bf16),
            pltpu.VMEM((chan_count // QUAD, QUAD, c_loc, nch), bf16),
            pltpu.VMEM((nch, nch), bf16),
            pltpu.VMEM((rows, nch, LANES), f32),
            dma, dma((2,)), dma((2,)), dma((2,)), dma, dma((2, chan_count // QUAD)), dma, dma,
        ],
        compiler_params=pltpu.CompilerParams(collective_id=0, has_side_effects=True),
        name="exchange_clean",
    )(visibility, eigen_basis, eigenvalues.reshape(1, nch), noise_power)


def turn(value, num, den):
    re, im = value
    num %= den
    eighth = 8 * num
    if num == 0:
        return re, im
    if eighth == 2 * den:
        return -im, re
    if eighth == 4 * den:
        return -re, -im
    if eighth == 6 * den:
        return im, -re
    angle = 2.0 * math.pi * num / den
    c, s = math.cos(angle), math.sin(angle)
    return re * c - im * s, re * s + im * c


def add(a, b):
    return a[0] + b[0], a[1] + b[1]


def sub(a, b):
    return a[0] - b[0], a[1] - b[1]


def inverse_fft(values):
    n = len(values)
    if n == 1:
        return values
    if n == 2:
        return [add(*values), sub(*values)]
    if n % 4 == 0 and n != 8:
        parts = [inverse_fft(values[k::4]) for k in range(4)]
        out = [None] * n
        for j in range(n // 4):
            a, b, c, d = (turn(parts[k][j], k * j, n) for k in range(4))
            ac, bd = add(a, c), add(b, d)
            am, bm = sub(a, c), turn(sub(b, d), 1, 4)
            out[j], out[j + n // 2] = add(ac, bd), sub(ac, bd)
            out[j + n // 4], out[j + 3 * n // 4] = add(am, bm), sub(am, bm)
        return out
    even, odd = inverse_fft(values[0::2]), inverse_fft(values[1::2])
    out = [None] * n
    for j in range(n // 2):
        o = turn(odd[j], j, n)
        out[j], out[j + n // 2] = add(even[j], o), sub(even[j], o)
    return out


def image_kernel(z, fb, fu, tw, out, zbuf, w, t, y_re, y_im, buf, sem_in, sem_out):
    rows, nv = z.shape[1], z.shape[2]
    outer = nv // LANES
    wide = 2 * LANES
    blocks = nv // wide
    f32, bf16 = jnp.float32, jnp.bfloat16

    def load(block):
        cols = pl.ds(pl.multiple_of(block * wide, wide), wide)
        return pltpu.make_async_copy(z.at[:, :, cols], zbuf.at[:, :, cols], sem_in.at[block])

    lax.fori_loop(0, blocks, lambda block, c: (load(block).start(), c)[1], 0)

    def row_stage(step, carry):
        for k in range(2):
            load(2 * step + k).wait()
        for k in range(2):
            cols = pl.ds(pl.multiple_of((2 * step + k) * wide, wide), wide)
            cells = jnp.concatenate([zbuf[0, :, cols], zbuf[1, :, cols]], axis=0)
            res = jnp.dot(fu[...], cells, preferred_element_type=f32)
            w[0, :, cols] = res[:rows]
            w[1, :, cols] = res[rows:]
        return carry

    lax.fori_loop(0, blocks // 2, row_stage, 0)

    def outer_stage(block, carry):
        r = pl.ds(pl.multiple_of(block * 8, 8), 8)
        values = [tuple(w[s, r, a * LANES:(a + 1) * LANES] for s in range(2)) for a in range(outer)]
        for j, (re, im) in enumerate(inverse_fft(values)):
            if j:
                c, s = tw[0, j:j + 1, :], tw[1, j:j + 1, :]
                re, im = re * c - im * s, re * s + im * c
            t[j, r, :LANES] = re
            t[j, r, LANES:] = im
        return carry

    lax.fori_loop(0, rows // 8, outer_stage, 0)

    pitch = outer + PAD

    def inner_stage(step, carry):
        results = []
        for k in range(INNER):
            cells = t[step * INNER + k].astype(bf16)
            results.append(jnp.dot(cells, fb[...], preferred_element_type=f32))
        for k, res in enumerate(results):
            to = pl.ds(step * INNER + k, LANES, stride=pitch)
            y_re[to, :] = jnp.transpose(res[:, :LANES])
            y_im[to, :] = jnp.transpose(res[:, LANES:])
        return carry

    lax.fori_loop(0, outer // INNER, inner_stage, 0)

    group = LANES // outer

    def out_stage(step, carry):
        for k in range(4):
            tile = step * 4 + k
            cols = pl.ds(pl.multiple_of(tile * LANES, LANES), LANES)
            for s, y in enumerate((y_re, y_im)):
                lines = [y[pl.ds((tile * group + g) * pitch, outer), :] for g in range(group)]
                buf[s, :, cols] = jnp.transpose(jnp.concatenate(lines, axis=0)).astype(bf16)
        cols = pl.ds(pl.multiple_of(step * 4 * LANES, 4 * LANES), 4 * LANES)
        pltpu.make_async_copy(buf.at[:, :, cols], out.at[:, 0, :, cols], sem_out).start()
        return carry

    lax.fori_loop(0, outer // 4, out_stage, 0)
    pltpu.make_async_copy(buf, out.at[:, 0], sem_out).wait()


def dft_matrix(n, scale):
    idx = np.outer(np.arange(n), np.arange(n)) % n
    c, s = np.cos(2 * np.pi * idx / n) * scale, np.sin(2 * np.pi * idx / n) * scale
    return np.block([[c, -s], [s, c]])


def image(z):
    _, rows, nv = z.shape
    outer = nv // LANES
    bf16, f32 = jnp.bfloat16, jnp.float32
    fb = jnp.asarray(dft_matrix(LANES, 1.0).T, bf16)
    fu = jnp.asarray(dft_matrix(rows, 1.0 / math.sqrt(rows * nv)), bf16)
    angle = 2 * np.pi * np.outer(np.arange(outer), np.arange(LANES)) / nv
    tw = jnp.asarray(np.stack([np.cos(angle), np.sin(angle)]), f32)
    vmem = pl.BlockSpec(memory_space=pltpu.VMEM)
    anywhere = pl.BlockSpec(memory_space=pl.ANY)
    lines = LANES * (outer + PAD)
    return pl.pallas_call(
        image_kernel,
        out_shape=jax.ShapeDtypeStruct((2, 1, rows, nv), bf16),
        in_specs=[anywhere, vmem, vmem, vmem],
        out_specs=anywhere,
        scratch_shapes=[
            pltpu.VMEM((2, rows, nv), bf16),
            pltpu.VMEM((2, rows, nv), f32),
            pltpu.VMEM((outer, rows, 2 * LANES), f32),
            pltpu.VMEM((lines, rows), f32), pltpu.VMEM((lines, rows), f32),
            pltpu.VMEM((2, rows, nv), bf16),
            pltpu.SemaphoreType.DMA((nv // (2 * LANES),)), pltpu.SemaphoreType.DMA,
        ],
        name="image",
    )(z, fb, fu, tw)


def shards(visibility, eigen_basis, eigenvalues, noise_power):
    z = exchange_and_clean(
        visibility, eigen_basis, eigenvalues, noise_power, lax.axis_size("uv"), lax.axis_size("chan")
    )
    return image(z)


def solution(mesh):
    in_specs = (P(None, "chan", "uv", None), P("chan", None), P(), P("uv"))
    out_specs = P(None, ("uv", "chan"), None, None)
    return jax.shard_map(shards, mesh=mesh, in_specs=in_specs, out_specs=out_specs, check_vma=False)
```

```python
import functools
import math

import jax
import jax.numpy as jnp
import numpy as np
from jax import lax
from jax.experimental import pallas as pl
from jax.experimental.pallas import tpu as pltpu
from jax.sharding import PartitionSpec as P

MESH = pl.DeviceIdType.MESH
LANES = 128
INNER = 8
PAD = 4
QUAD = 4


def ring_offset(step):
    return ((step + 1) // 2) * (1 if step % 2 else -1)


def clean_kernel(uv_count, chan_count, vis, eb, values, noise, z, d_in, work, c_out, held, mid, basis, basis_t, gains,
                 s_vis, r_vis, s_eb, r_eb, s_uv, r_uv, s_held, s_back, r_back, s_fin, r_fin):
    uv = lax.axis_index("uv")
    ch = lax.axis_index("chan")
    ring = chan_count // QUAD
    y, q = ch // QUAD, ch % QUAD
    c_loc = vis.shape[1]
    rows = vis.shape[2]
    zring = uv_count // 2
    xh, zz = uv // zring, uv % zring

    def chan_peer(step, m):
        return ((y + ring_offset(step) + ring) % ring) * QUAD + (q + m) % QUAD

    def uv_peer(step, m):
        return ((xh + m) % 2) * zring + (zz + ring_offset(step) + zring) % zring

    chan_steps = [(t, m) for t in range(ring) for m in range(QUAD)]
    uv_steps = [(0, 0)] + [(t, m) for t in reversed(range(zring)) for m in range(2) if t or m]

    barrier = pltpu.get_barrier_semaphore()
    for t, m in chan_steps[1:]:
        pl.semaphore_signal(barrier, inc=1, device_id=(uv, chan_peer(t, m)), device_id_type=MESH)
    for t, m in uv_steps[1:]:
        pl.semaphore_signal(barrier, inc=1, device_id=(uv_peer(t, m), ch), device_id_type=MESH)
    pl.semaphore_wait(barrier, chan_count - 1 + uv_count - 1)

    for t in range(1, ring):
        pltpu.make_async_remote_copy(
            eb, basis.at[y, q], s_eb.at[0], r_eb.at[0], device_id=(uv, chan_peer(t, 0)), device_id_type=MESH
        ).start()
    pltpu.make_async_copy(eb, basis.at[y, q], r_eb.at[0]).start()

    def send_vis(s, steps):
        for t, m in steps:
            p = chan_peer(t, m)
            src = vis.at[s, :, :, pl.ds(pl.multiple_of(p * LANES, LANES), LANES)]
            dst = d_in.at[s, pl.ds(ch * c_loc, c_loc)]
            if (t, m) == (0, 0):
                pltpu.make_async_copy(src, dst, r_vis.at[s]).start()
            else:
                pltpu.make_async_remote_copy(
                    src, dst, s_vis, r_vis.at[s], device_id=(uv, p), device_id_type=MESH
                ).start()

    for s in range(2):
        send_vis(s, chan_steps)

    nch = basis_t.shape[0]
    spread = jnp.transpose(jnp.broadcast_to(values[...], (LANES, nch)))
    for u in range(rows):
        gains[u] = spread / (spread + noise[u])

    pltpu.make_async_copy(basis.at[:, q], basis.at[:, q], r_eb.at[0]).wait()
    for m in range(1, QUAD):
        pltpu.make_async_remote_copy(
            basis.at[:, q], basis.at[:, q], s_eb.at[1], r_eb.at[1],
            device_id=(uv, chan_peer(0, m)), device_id_type=MESH,
        ).start()
    pltpu.make_async_copy(basis.at[:, pl.ds(0, QUAD - 1)], basis.at[:, pl.ds(0, QUAD - 1)], r_eb.at[1]).wait()
    basis_t[...] = jnp.transpose(basis[...].reshape(nch, nch).astype(jnp.float32)).astype(jnp.bfloat16)

    def clean(s):
        pltpu.make_async_copy(d_in.at[s], d_in.at[s], r_vis.at[s]).wait()
        work[...] = d_in[s].astype(jnp.float32).reshape(nch * rows, LANES)

        def clean_pair(pair, carry):
            first = pl.ds(2 * pair, nch, stride=rows)
            second = pl.ds(2 * pair + 1, nch, stride=rows)
            cells = jnp.concatenate([work[first, :], work[second, :]], axis=1)
            amps = jnp.dot(basis_t[...], cells.astype(jnp.bfloat16), preferred_element_type=jnp.float32)
            gain_pair = jnp.concatenate([gains[2 * pair], gains[2 * pair + 1]], axis=1)
            fore = (gain_pair * amps.astype(jnp.bfloat16).astype(jnp.float32)).astype(jnp.bfloat16)
            slab = jnp.dot(basis[...].reshape(nch, nch), fore, preferred_element_type=jnp.float32)
            left = cells - slab
            work[first, :] = left[:, :LANES]
            work[second, :] = left[:, LANES:]
            return carry

        lax.fori_loop(0, rows // 2, clean_pair, 0)
        c_out[s] = work[...].astype(jnp.bfloat16).reshape(c_out.shape[1:])

    def send_uv():
        for m in range(2):
            for t, mm in uv_steps:
                if mm != m:
                    continue
                p = uv_peer(t, m)
                if (t, m) == (0, 0):
                    pltpu.make_async_copy(c_out.at[0, uv], held.at[uv], r_uv.at[m]).start()
                else:
                    pltpu.make_async_remote_copy(
                        c_out.at[0, p], held.at[uv], s_uv, r_uv.at[m], device_id=(p, ch), device_id_type=MESH
                    ).start()

    lanes = pl.ds(pl.multiple_of(ch * LANES, LANES), LANES)

    def relay_chan(m):
        some = pl.ds(((xh + m) % 2) * zring, zring)
        pltpu.make_async_copy(held.at[some], held.at[some], r_uv.at[m]).wait()
        for t, k in chan_steps:
            p = chan_peer(t, k)
            to = z.at[0, some, :, lanes]
            if (t, k) == (0, 0):
                pltpu.make_async_copy(held.at[some, ch], to, r_fin).start()
            else:
                pltpu.make_async_remote_copy(
                    held.at[some, p], to, s_held, r_fin, device_id=(uv, p), device_id_type=MESH
                ).start()

    def send_back():
        for t, m in chan_steps:
            p = chan_peer(t, m)
            if (t, m) == (0, 0):
                pltpu.make_async_copy(c_out.at[1, :, ch], mid.at[:, :, lanes], r_back.at[y]).start()
            else:
                pltpu.make_async_remote_copy(
                    c_out.at[1, :, p], mid.at[:, :, lanes], s_back, r_back.at[y],
                    device_id=(uv, p), device_id_type=MESH,
                ).start()

    width = QUAD * LANES

    def relay_uv(t):
        src = (y + ring_offset(t) + ring) % ring
        cols = pl.ds(pl.multiple_of(src * width, width), width)
        pltpu.make_async_copy(mid.at[:, :, cols], mid.at[:, :, cols], r_back.at[src]).wait()
        for tt, m in uv_steps:
            p = uv_peer(tt, m)
            to = z.at[1, uv, :, cols]
            if (tt, m) == (0, 0):
                pltpu.make_async_copy(mid.at[uv, :, cols], to, r_fin).start()
            else:
                pltpu.make_async_remote_copy(
                    mid.at[p, :, cols], to, s_fin, r_fin, device_id=(p, ch), device_id_type=MESH
                ).start()

    clean(0)
    send_uv()
    relay_chan(0)
    clean(1)
    send_back()
    relay_chan(1)
    for t in range(ring):
        relay_uv(t)

    pltpu.make_async_copy(z, z, r_fin).wait()
    for gone, sem in (
        (d_in.at[:, pl.ds(0, (chan_count - 1) * c_loc)], s_vis),
        (c_out.at[0, pl.ds(0, uv_count - 1)], s_uv),
        (held.at[:, pl.ds(0, chan_count - 1)], s_held),
        (c_out.at[1, :, pl.ds(0, chan_count - 1)], s_back),
        (mid.at[pl.ds(0, uv_count - 1)], s_fin),
        (basis.at[pl.ds(0, ring - 1), 0], s_eb.at[0]),
        (basis.at[:, pl.ds(0, QUAD - 1)], s_eb.at[1]),
    ):
        pltpu.make_async_copy(gone, gone, sem).wait()


def exchange_and_clean(visibility, eigen_basis, eigenvalues, noise_power, uv_count, chan_count):
    _, c_loc, rows, nv = visibility.shape
    nch = c_loc * chan_count
    bf16, f32 = jnp.bfloat16, jnp.float32
    vmem = pl.BlockSpec(memory_space=pltpu.VMEM)
    dma = pltpu.SemaphoreType.DMA
    return pl.pallas_call(
        functools.partial(clean_kernel, uv_count, chan_count),
        out_shape=jax.ShapeDtypeStruct((2, uv_count, rows, nv), bf16),
        in_specs=[pl.BlockSpec(memory_space=pl.ANY), vmem, vmem, pl.BlockSpec(memory_space=pltpu.SMEM)],
        out_specs=pl.BlockSpec(memory_space=pl.ANY),
        scratch_shapes=[
            pltpu.VMEM((2, nch, rows, LANES), bf16),
            pltpu.VMEM((nch * rows, LANES), f32),
            pltpu.VMEM((2, uv_count, chan_count, rows, LANES), bf16),
            pltpu.VMEM((uv_count, chan_count, rows, LANES), bf16),
            pltpu.VMEM((uv_count, rows, nv), bf16),
            pltpu.VMEM((chan_count // QUAD, QUAD, c_loc, nch), bf16),
            pltpu.VMEM((nch, nch), bf16),
            pltpu.VMEM((rows, nch, LANES), f32),
            dma, dma((2,)), dma((2,)), dma((2,)), dma, dma((2,)), dma, dma, dma((chan_count // QUAD,)), dma, dma,
        ],
        compiler_params=pltpu.CompilerParams(collective_id=0, has_side_effects=True),
        name="exchange_clean",
    )(visibility, eigen_basis, eigenvalues.reshape(1, nch), noise_power).reshape(2, uv_count * rows, nv)


def turn(value, num, den):
    re, im = value
    num %= den
    eighth = 8 * num
    if num == 0:
        return re, im
    if eighth == 2 * den:
        return -im, re
    if eighth == 4 * den:
        return -re, -im
    if eighth == 6 * den:
        return im, -re
    angle = 2.0 * math.pi * num / den
    c, s = math.cos(angle), math.sin(angle)
    return re * c - im * s, re * s + im * c


def add(a, b):
    return a[0] + b[0], a[1] + b[1]


def sub(a, b):
    return a[0] - b[0], a[1] - b[1]


def inverse_fft(values):
    n = len(values)
    if n == 1:
        return values
    if n == 2:
        return [add(*values), sub(*values)]
    if n % 4 == 0 and n != 8:
        parts = [inverse_fft(values[k::4]) for k in range(4)]
        out = [None] * n
        for j in range(n // 4):
            a, b, c, d = (turn(parts[k][j], k * j, n) for k in range(4))
            ac, bd = add(a, c), add(b, d)
            am, bm = sub(a, c), turn(sub(b, d), 1, 4)
            out[j], out[j + n // 2] = add(ac, bd), sub(ac, bd)
            out[j + n // 4], out[j + 3 * n // 4] = add(am, bm), sub(am, bm)
        return out
    even, odd = inverse_fft(values[0::2]), inverse_fft(values[1::2])
    out = [None] * n
    for j in range(n // 2):
        o = turn(odd[j], j, n)
        out[j], out[j + n // 2] = add(even[j], o), sub(even[j], o)
    return out


def image_kernel(z, fb, fu, tw, out, zbuf, w, t, y_re, y_im, buf, sem_in, sem_out):
    rows, nv = z.shape[1], z.shape[2]
    outer = nv // LANES
    wide = 2 * LANES
    blocks = nv // wide
    f32, bf16 = jnp.float32, jnp.bfloat16

    def load(block):
        cols = pl.ds(pl.multiple_of(block * wide, wide), wide)
        return pltpu.make_async_copy(z.at[:, :, cols], zbuf.at[:, :, cols], sem_in.at[block])

    lax.fori_loop(0, blocks, lambda block, c: (load(block).start(), c)[1], 0)

    def row_stage(step, carry):
        for k in range(2):
            load(2 * step + k).wait()
        for k in range(2):
            cols = pl.ds(pl.multiple_of((2 * step + k) * wide, wide), wide)
            cells = jnp.concatenate([zbuf[0, :, cols], zbuf[1, :, cols]], axis=0)
            res = jnp.dot(fu[...], cells, preferred_element_type=f32)
            w[0, :, cols] = res[:rows]
            w[1, :, cols] = res[rows:]
        return carry

    lax.fori_loop(0, blocks // 2, row_stage, 0)

    def outer_stage(block, carry):
        r = pl.ds(pl.multiple_of(block * 8, 8), 8)
        values = [tuple(w[s, r, a * LANES:(a + 1) * LANES] for s in range(2)) for a in range(outer)]
        for j, (re, im) in enumerate(inverse_fft(values)):
            if j:
                c, s = tw[0, j:j + 1, :], tw[1, j:j + 1, :]
                re, im = re * c - im * s, re * s + im * c
            t[j, r, :LANES] = re
            t[j, r, LANES:] = im
        return carry

    lax.fori_loop(0, rows // 8, outer_stage, 0)

    pitch = outer + PAD

    def inner_stage(step, carry):
        results = []
        for k in range(INNER):
            cells = t[step * INNER + k].astype(bf16)
            results.append(jnp.dot(cells, fb[...], preferred_element_type=f32))
        for k, res in enumerate(results):
            to = pl.ds(step * INNER + k, LANES, stride=pitch)
            y_re[to, :] = jnp.transpose(res[:, :LANES].astype(bf16)).astype(f32)
            y_im[to, :] = jnp.transpose(res[:, LANES:].astype(bf16)).astype(f32)
        return carry

    lax.fori_loop(0, outer // INNER, inner_stage, 0)

    group = LANES // outer

    def out_stage(step, carry):
        for k in range(4):
            tile = step * 4 + k
            cols = pl.ds(pl.multiple_of(tile * LANES, LANES), LANES)
            for s, y in enumerate((y_re, y_im)):
                lines = [y[pl.ds((tile * group + g) * pitch, outer), :] for g in range(group)]
                buf[s, :, cols] = jnp.transpose(jnp.concatenate(lines, axis=0)).astype(bf16)
        cols = pl.ds(pl.multiple_of(step * 4 * LANES, 4 * LANES), 4 * LANES)
        pltpu.make_async_copy(buf.at[:, :, cols], out.at[:, 0, :, cols], sem_out).start()
        return carry

    lax.fori_loop(0, outer // 4, out_stage, 0)
    pltpu.make_async_copy(buf, out.at[:, 0], sem_out).wait()


def dft_matrix(n, scale):
    idx = np.outer(np.arange(n), np.arange(n)) % n
    c, s = np.cos(2 * np.pi * idx / n) * scale, np.sin(2 * np.pi * idx / n) * scale
    return np.block([[c, -s], [s, c]])


def image(z):
    _, rows, nv = z.shape
    outer = nv // LANES
    bf16, f32 = jnp.bfloat16, jnp.float32
    fb = jnp.asarray(dft_matrix(LANES, 1.0).T, bf16)
    fu = jnp.asarray(dft_matrix(rows, 1.0 / math.sqrt(rows * nv)), bf16)
    angle = 2 * np.pi * np.outer(np.arange(outer), np.arange(LANES)) / nv
    tw = jnp.asarray(np.stack([np.cos(angle), np.sin(angle)]), f32)
    vmem = pl.BlockSpec(memory_space=pltpu.VMEM)
    anywhere = pl.BlockSpec(memory_space=pl.ANY)
    lines = LANES * (outer + PAD)
    return pl.pallas_call(
        image_kernel,
        out_shape=jax.ShapeDtypeStruct((2, 1, rows, nv), bf16),
        in_specs=[anywhere, vmem, vmem, vmem],
        out_specs=anywhere,
        scratch_shapes=[
            pltpu.VMEM((2, rows, nv), bf16),
            pltpu.VMEM((2, rows, nv), f32),
            pltpu.VMEM((outer, rows, 2 * LANES), f32),
            pltpu.VMEM((lines, rows), f32), pltpu.VMEM((lines, rows), f32),
            pltpu.VMEM((2, rows, nv), bf16),
            pltpu.SemaphoreType.DMA((nv // (2 * LANES),)), pltpu.SemaphoreType.DMA,
        ],
        name="image",
    )(z, fb, fu, tw)


def shards(visibility, eigen_basis, eigenvalues, noise_power):
    z = exchange_and_clean(
        visibility, eigen_basis, eigenvalues, noise_power, lax.axis_size("uv"), lax.axis_size("chan")
    )
    return image(z)


def solution(mesh):
    in_specs = (P(None, "chan", "uv", None), P("chan", None), P(), P("uv"))
    out_specs = P(None, ("uv", "chan"), None, None)
    return jax.shard_map(shards, mesh=mesh, in_specs=in_specs, out_specs=out_specs, check_vma=False)
```
